32 devices in a mesh: body: 4 (over y, core), surf: 8 (over z, x).
Axes of the slice: x: 2, y: 2, z: 4, core: 2. Of those that a mesh axis runs over, the one named last changes fastest.
Arguments:
- external_load: float32 [3, 32, 128, 1024], P(None, 'body', 'surf'), may hold values from -18 to 18
- modulus: float32 [32, 128, 1024], P('body', 'surf'), may hold values from 0.2 to 10, as said below
- active: int32 [128, 1024], P('surf'), may hold values 0 or 1
Outputs:
- lam_depth: float32 [3, 4, 128, 1024], P(None, 'body', 'surf')
- lam_surface: float32 [3, 32, 8, 1024], P(None, 'body', 'surf')
- lam_contact: float32 [4, 128, 1024], P('body', 'surf')
The draws below stay inside these ranges and needn't reach their ends.
Inputs may be any that keep to these rules, and one draw needn't show every extreme that they name: The modulus is positive.
All inputs are finite; a program needn't handle non-finite values. No bound on the sum of `active` on one device may be relied on, other than what follows from the above.
Results may differ from the reference program's by a relative error of at most 0.0003.
Values sent between devices are 32-bit elements; how exact they have to be, the bound alone decides.
A program may use at most 192 MiB of HBM per device.

```python
import math
import jax
import jax.numpy as jnp
from jax import lax

SX = 8
SY = 16
SZ = 1024
ITERS = 3
SWEEPS = 6
NX = 32
NY = 128
N_BODY = 4
N_SURF = 8


def draw_external_load(key, part):
    rough_key = jax.random.fold_in(jax.random.fold_in(key, 11), 0)
    depth_rise = (jnp.arange(NX, dtype=jnp.float32) / NX)[None, :, None, None]
    across_rise = (jnp.arange(NY, dtype=jnp.float32) / NY)[None, None, :, None]
    scale_field = 0.5 * (1.0 + 2.0 * depth_rise) * (1.0 + 2.0 * across_rise)
    rough = jnp.clip(jax.random.normal(rough_key, (3, NX, NY, SZ), jnp.float32), -4.0, 4.0)
    return rough * scale_field


def draw_modulus(key, part):
    layer_key, node_key = jax.random.split(jax.random.fold_in(key, 23))
    layers = jnp.exp(jax.random.uniform(layer_key, (NX, 1, 1), jnp.float32, math.log(0.5), math.log(4.0)))
    nodes = jnp.exp(jax.random.uniform(node_key, (NX, NY, SZ), jnp.float32, math.log(0.4), math.log(2.5)))
    return layers * nodes


def place_ends(entries, stream_key, smallest, top_value):
    place = [jax.random.randint(jax.random.fold_in(stream_key, axis), (), 0, length) for axis, length in enumerate(entries.shape)]
    widest = entries.shape.index(max(entries.shape))
    next_to = place[:widest] + [(place[widest] + 1) % entries.shape[widest]] + place[widest + 1:]
    return entries.at[tuple(place)].set(smallest).at[tuple(next_to)].set(top_value)


def setup_inputs(seed: int = 0) -> dict:
    seeds = jax.random.split(jax.random.key(seed), 4)
    external_load = draw_external_load(jax.random.fold_in(seeds[3], 71), 0)
    modulus = draw_modulus(jax.random.fold_in(seeds[3], 71), 0)
    active = place_ends((jax.random.randint(seeds[2], (NY, SZ), 0, 2) < 1).astype(jnp.int32), jax.random.fold_in(seeds[2], 1), 0, 1)
    return {"external_load": external_load, "modulus": modulus, "active": active}


OFFSETS = [(plane_x, plane_y, plane_z) for plane_x in (-1, 0, 1) for plane_y in (-1, 0, 1) for plane_z in (-1, 0, 1) if (plane_x, plane_y, plane_z) != (0, 0, 0)]
COUPLING_SCALE = (0.0, 1.0, 0.5, 0.25)
RELAXATION = 0.6

def coupling(modulus, padded, offset):
    cells_x, cells_y, cells_z = modulus.shape
    nearby = padded[1 + offset[0]:1 + offset[0] + cells_x, 1 + offset[1]:1 + offset[1] + cells_y, 1 + offset[2]:1 + offset[2] + cells_z]
    weight = COUPLING_SCALE[abs(offset[0]) + abs(offset[1]) + abs(offset[2])]
    return weight * 2.0 * modulus * nearby / (modulus + nearby)

def inexact_solve(source, modulus):
    cells_x, cells_y, cells_z = modulus.shape
    padded = jnp.pad(modulus, 1)
    weights = [coupling(modulus, padded, offset) for offset in OFFSETS]
    diagonal = jnp.zeros_like(modulus)
    for weight_field in weights:
        diagonal = diagonal + weight_field
    iterate = RELAXATION * source / diagonal
    for repeat in range(SWEEPS - 1):
        spread = jnp.pad(iterate, ((0, 0), (1, 1), (1, 1), (1, 1)))
        applied = diagonal * iterate
        for offset, weight_field in zip(OFFSETS, weights):
            neighbour = spread[:, 1 + offset[0]:1 + offset[0] + cells_x, 1 + offset[1]:1 + offset[1] + cells_y, 1 + offset[2]:1 + offset[2] + cells_z]
            applied = applied - weight_field * neighbour
        iterate = iterate + RELAXATION * (source - applied) / diagonal
    return iterate

def coarse_factors(counts, n_depth, n_across, face_x, face_y):
    eye_depth = jnp.eye(n_depth, dtype=jnp.float32)
    path_matrix = 2.0 * eye_depth - jnp.eye(n_depth, k=1, dtype=jnp.float32) - jnp.eye(n_depth, k=-1, dtype=jnp.float32)
    path_matrix = path_matrix.at[0, 0].set(1.0)
    eye_across = jnp.eye(n_across, dtype=jnp.float32)
    cycle_matrix = 2.0 * eye_across - jnp.roll(eye_across, 1, axis=1) - jnp.roll(eye_across, -1, axis=1)
    base_matrix = face_x * jnp.kron(path_matrix, eye_across) + face_y * jnp.kron(eye_depth, cycle_matrix)
    normal_factor = jnp.linalg.cholesky(base_matrix + jnp.diag(counts))
    tangent_factor = jnp.linalg.cholesky(base_matrix)
    return (normal_factor, tangent_factor)

def coarse_solve(normal_factor, tangent_factor, coarse_rhs):
    normal_part = jax.scipy.linalg.cho_solve((normal_factor, True), coarse_rhs[0])
    tangent_part = jax.scipy.linalg.cho_solve((tangent_factor, True), coarse_rhs[1:].T).T
    return jnp.concatenate([normal_part[None], tangent_part], 0)

def transpose_apply(upper, lower, right_face, left_face, contact, mask_face, cells_x, cells_y):
    field = jnp.zeros((3, cells_x, cells_y, upper.shape[-1]), jnp.float32)
    field = field.at[:, cells_x - 1].add(upper)
    field = field.at[:, 0].add(-lower)
    field = field.at[:, :, cells_y - 1].add(right_face)
    field = field.at[:, :, 0].add(-left_face)
    field = field.at[0, 0].add(-contact * mask_face)
    return field

def reference(external_load, modulus, active):
    n_depth, n_across = (N_BODY, N_SURF)
    count_sub = n_depth * n_across
    load_blocks = external_load.reshape(3, n_depth, SX, n_across, SY, SZ).transpose(1, 3, 0, 2, 4, 5).reshape(count_sub, 3, SX, SY, SZ)
    modulus_blocks = modulus.reshape(n_depth, SX, n_across, SY, SZ).transpose(0, 2, 1, 3, 4).reshape(count_sub, SX, SY, SZ)
    mask_full = jnp.zeros((n_depth, n_across, SY, SZ), jnp.float32).at[0].set(active.astype(jnp.float32).reshape(n_across, SY, SZ))
    counts = jnp.sum(mask_full, axis=(2, 3)).reshape(count_sub)
    normal_factor, tangent_factor = coarse_factors(counts, n_depth, n_across, float(SY * SZ), float(SX * SZ))

    def lift(coarse_alpha):
        grid_alpha = coarse_alpha.reshape(3, n_depth, n_across).transpose(1, 2, 0)
        above = jnp.concatenate([grid_alpha[1:], jnp.zeros_like(grid_alpha[:1])], 0)
        right_alpha = jnp.roll(grid_alpha, -1, axis=1)
        depth_rows = jnp.broadcast_to((grid_alpha - above)[:, :, :, None, None], (n_depth, n_across, 3, SY, SZ))
        across_rows = jnp.broadcast_to((grid_alpha - right_alpha)[:, :, :, None, None], (n_depth, n_across, 3, SX, SZ))
        contact_rows = -grid_alpha[:, :, 0][:, :, None, None] * mask_full
        return (depth_rows, across_rows, contact_rows)

    def restrict(vector):
        sums_x = jnp.sum(vector[0], axis=(3, 4))
        sums_y = jnp.sum(vector[1], axis=(3, 4))
        sums_c = jnp.sum(vector[2], axis=(2, 3))
        below = jnp.concatenate([jnp.zeros_like(sums_x[:1]), sums_x[:-1]], 0)
        totals = sums_x - below + sums_y - jnp.roll(sums_y, 1, axis=1)
        totals = totals.at[:, :, 0].add(-sums_c)
        return totals.transpose(2, 0, 1).reshape(3, count_sub)

    def inner(first, second):
        return jnp.sum(first[0] * second[0]) + jnp.sum(first[1] * second[1]) + jnp.sum(first[2] * second[2])

    def combine(first, second, factor):
        return tuple((left_part + factor * right_part for left_part, right_part in zip(first, second)))

    def project(vector):
        coarse_alpha = coarse_solve(normal_factor, tangent_factor, restrict(vector))
        return combine(vector, lift(coarse_alpha), -1.0)

    def traces(vector, with_load):
        lower = jnp.concatenate([jnp.zeros_like(vector[0][:1]), vector[0][:-1]], 0)
        left_rows = jnp.roll(vector[1], 1, axis=1)
        pieces = (vector[0], lower, vector[1], left_rows, vector[2], mask_full)
        flat = tuple((piece.reshape((count_sub,) + piece.shape[2:]) for piece in pieces)) + (modulus_blocks, load_blocks)

        def one_block(items):
            field = transpose_apply(items[0], items[1], items[2], items[3], items[4], items[5], SX, SY)
            source = items[7] - field if with_load else field
            solved = inexact_solve(source, items[6])
            return (solved[:, 0], solved[:, SX - 1], solved[:, :, 0], solved[:, :, SY - 1])
        outputs = lax.map(one_block, flat)
        return tuple((piece.reshape((n_depth, n_across) + piece.shape[1:]) for piece in outputs))

    def jumps(first_x, last_x, first_y, last_y):
        above = jnp.concatenate([first_x[1:], jnp.zeros_like(first_x[:1])], 0)
        return (last_x - above, last_y - jnp.roll(first_y, -1, axis=1), -first_x[:, :, 0] * mask_full)
    load_sums = jnp.sum(load_blocks, axis=(2, 3, 4)).T
    multipliers = lift(coarse_solve(normal_factor, tangent_factor, load_sums))
    gradient = tuple((-piece for piece in jumps(*traces(multipliers, True))))
    projected = project(gradient)
    norm_now = inner(projected, projected)
    direction = projected
    for step_index in range(ITERS):
        image = jumps(*traces(direction, False))
        step_size = norm_now / inner(direction, image)
        multipliers = combine(multipliers, direction, step_size)
        if step_index + 1 < ITERS:
            gradient = combine(gradient, image, step_size)
            projected = project(gradient)
            norm_next = inner(projected, projected)
            direction = combine(projected, direction, norm_next / norm_now)
            norm_now = norm_next
    lam_depth = multipliers[0].transpose(2, 0, 1, 3, 4).reshape(3, n_depth, n_across * SY, SZ)
    lam_surface = multipliers[1].transpose(2, 0, 3, 1, 4).reshape(3, n_depth * SX, n_across, SZ)
    lam_contact = multipliers[2].reshape(n_depth, n_across * SY, SZ)
    return (lam_depth, lam_surface, lam_contact)
```

```python
import functools

import jax
import jax.numpy as jnp
import numpy as np
from jax import lax
from jax.experimental import pallas as pl
from jax.experimental.pallas import tpu as pltpu
from jax.sharding import PartitionSpec as P

ITERS = 3
SWEEPS = 6
COUPLING_SCALE = (0.0, 1.0, 0.5, 0.25)
RELAXATION = 0.6
PLANE = [(dx, dy) for dx in (-1, 0, 1) for dy in (-1, 0, 1)]
SAME = [o for o in PLANE if o != (0, 0)]
SUB, LANE = 8, 128


def shift_up(t):
    lane = lax.broadcasted_iota(jnp.int32, t.shape, 1)
    r = pltpu.roll(t, 1, 1)
    return jnp.where(lane == 0, pltpu.roll(r, 1, 0), r)


def shift_down(t):
    lane = lax.broadcasted_iota(jnp.int32, t.shape, 1)
    r = pltpu.roll(t, LANE - 1, 1)
    return jnp.where(lane == LANE - 1, pltpu.roll(r, SUB - 1, 0), r)


def setup_weights(nx, ny, mod_ref, mp, w_ref, q_ref):
    zero = jnp.zeros((SUB, LANE), jnp.float32)

    def clear(y, c):
        mp[0, y] = zero
        mp[nx + 1, y] = zero
        return c

    lax.fori_loop(0, ny + 2, clear, 0)

    def fill(x, c):
        mp[x + 1, 0] = zero
        mp[x + 1, ny + 1] = zero
        mp[x + 1, pl.ds(1, ny)] = mod_ref[x]
        return c

    lax.fori_loop(0, nx, fill, 0)
    sub = lax.broadcasted_iota(jnp.int32, (SUB, LANE), 0)
    lane = lax.broadcasted_iota(jnp.int32, (SUB, LANE), 1)
    first = (sub == 0) & (lane == 0)
    last = (sub == SUB - 1) & (lane == LANE - 1)

    def column(i, c):
        x = i // ny
        y = i % ny
        a = mp[x + 1, y + 1]
        up = jnp.where(first, 0.0, shift_up(a))
        down = jnp.where(last, 0.0, shift_down(a))
        total0 = zero
        total_p = zero
        total_m = zero
        for dx, dy in PLANE:
            b = mp[x + 1 + dx, y + 1 + dy]
            k = abs(dx) + abs(dy)
            if k:
                w = (2.0 * COUPLING_SCALE[k]) * a * b / (a + b)
                w_ref[SAME.index((dx, dy)), x, y] = w
                total0 = total0 + w
            scale = 2.0 * COUPLING_SCALE[k + 1]
            j = PLANE.index((dx, dy))
            w = scale * up * b / jnp.maximum(up + b, 1e-30)
            w_ref[8 + j, x, y] = w
            total_p = total_p + w
            w = scale * down * b / jnp.maximum(down + b, 1e-30)
            w_ref[17 + j, x, y] = w
            total_m = total_m + w
        diag = total0 + shift_down(total_p) + shift_up(total_m)
        q_ref[x, y] = RELAXATION / diag
        return c

    lax.fori_loop(0, nx * ny, column, 0)


def column_update(x, y, src, dst, s_ref, w_ref, q_ref):
    center, plus, minus, mid = [], [], [], []
    for comp in range(3):
        mid.append(s_ref[comp, x, y])
    for n, (dx, dy) in enumerate(PLANE):
        wp = w_ref[8 + n, x, y]
        wm = w_ref[17 + n, x, y]
        w0 = w_ref[SAME.index((dx, dy)), x, y] if (dx, dy) != (0, 0) else None
        for comp in range(3):
            v = src[comp, x + 1 + dx, y + 1 + dy]
            if n == 0:
                plus.append(wp * v)
                minus.append(wm * v)
            else:
                plus[comp] = plus[comp] + wp * v
                minus[comp] = minus[comp] + wm * v
            if w0 is None:
                center.append(v)
            else:
                mid[comp] = mid[comp] + w0 * v
    q = q_ref[x, y]
    for comp in range(3):
        total = mid[comp] + shift_down(plus[comp]) + shift_up(minus[comp])
        dst[comp, x + 1, y + 1] = (1.0 - RELAXATION) * center[comp] + q * total


def sweep(nx, ny, depth, src, dst, s_ref, w_ref, q_ref):
    full = min(nx, 2 * (depth + 1))
    step = 4

    def rows(i, c):
        r = i // (ny // step)
        y0 = (i % (ny // step)) * step
        x = r if full == nx else jnp.where(r <= depth, r, r + (nx - full))
        for j in range(step):
            column_update(x, y0 + j, src, dst, s_ref, w_ref, q_ref)
        return c

    lax.fori_loop(0, full * (ny // step), rows, 0)
    if full < nx:
        def sides(i, c):
            x = depth + 1 + i
            for j in range(depth + 1):
                column_update(x, j, src, dst, s_ref, w_ref, q_ref)
                column_update(x, ny - 1 - j, src, dst, s_ref, w_ref, q_ref)
            return c

        lax.fori_loop(0, nx - full, sides, 0)


def relax(nx, ny, local, va, vb, s_ref, w_ref, q_ref):
    deepest = (min(nx, ny) - 1) // 2

    def start(x, c):
        for comp in range(3):
            va[comp, x + 1, pl.ds(1, ny)] = q_ref[x] * s_ref[comp, x]
            if local:
                vb[comp, x + 1, pl.ds(1, ny)] = jnp.zeros((ny, SUB, LANE), jnp.float32)
        return c

    lax.fori_loop(0, nx, start, 0)
    bufs = (va, vb)
    for k in range(1, SWEEPS):
        depth = min(deepest, SWEEPS - 1 - k)
        if local:
            depth = min(depth, k)
        sweep(nx, ny, depth, bufs[(k - 1) % 2], bufs[k % 2], s_ref, w_ref, q_ref)
    return bufs[(SWEEPS - 1) % 2]


def clear_halo(nx, ny, va, vb):
    zero = jnp.zeros((SUB, LANE), jnp.float32)
    for v in (va, vb):
        for comp in range(3):
            v[comp, 0] = jnp.zeros((ny + 2, SUB, LANE), jnp.float32)
            v[comp, nx + 1] = jnp.zeros((ny + 2, SUB, LANE), jnp.float32)

            def side(x, c):
                v[comp, x + 1, 0] = zero
                v[comp, x + 1, ny + 1] = zero
                return c

            lax.fori_loop(0, nx, side, 0)


def add_faces(nx, ny, s_ref, own_x, up_x, own_y, left_y, contact, mask, sign):
    for comp in range(3):
        s_ref[comp, nx - 1] = s_ref[comp, nx - 1] + sign * own_x[comp]
        s_ref[comp, 0] = s_ref[comp, 0] - sign * up_x[comp]

        def side(x, c):
            s_ref[comp, x, ny - 1] = s_ref[comp, x, ny - 1] + sign * own_y[comp, x]
            s_ref[comp, x, 0] = s_ref[comp, x, 0] - sign * left_y[comp, x]
            return c

        lax.fori_loop(0, nx, side, 0)
    s_ref[0, 0] = s_ref[0, 0] - sign * contact[...] * mask[...]


def take_faces(nx, ny, v, first_x, last_x, first_y, last_y):
    for comp in range(3):
        first_x[comp] = v[comp, 1, pl.ds(1, ny)]
        last_x[comp] = v[comp, nx, pl.ds(1, ny)]

        def side(x, c):
            first_y[comp, x] = v[comp, x + 1, 1]
            last_y[comp, x] = v[comp, x + 1, ny]
            return c

        lax.fori_loop(0, nx, side, 0)


def load_kernel(nx, ny, load, mod, own_x, up_x, own_y, left_y, contact, mask,
                w_ref, q_ref, first_x, last_x, first_y, last_y, mp, va, vb, s_ref):
    setup_weights(nx, ny, mod, mp, w_ref, q_ref)
    clear_halo(nx, ny, va, vb)
    s_ref[...] = load[...]
    add_faces(nx, ny, s_ref, own_x, up_x, own_y, left_y, contact, mask, -1.0)
    v = relax(nx, ny, False, va, vb, s_ref, w_ref, q_ref)
    take_faces(nx, ny, v, first_x, last_x, first_y, last_y)


def direction_kernel(nx, ny, w_ref, q_ref, own_x, up_x, own_y, left_y, contact, mask,
                     first_x, last_x, first_y, last_y, va, vb, s_ref):
    clear_halo(nx, ny, va, vb)
    s_ref[...] = jnp.zeros_like(s_ref)
    add_faces(nx, ny, s_ref, own_x, up_x, own_y, left_y, contact, mask, 1.0)
    v = relax(nx, ny, True, va, vb, s_ref, w_ref, q_ref)
    take_faces(nx, ny, v, first_x, last_x, first_y, last_y)


def coarse_constants(n_depth, n_across, face_x, face_y):
    path = 2.0 * np.eye(n_depth) - np.eye(n_depth, k=1) - np.eye(n_depth, k=-1)
    path[0, 0] = 1.0
    eye = np.eye(n_across)
    cycle = 2.0 * eye - np.roll(eye, 1, axis=1) - np.roll(eye, -1, axis=1)
    base = face_x * np.kron(path, eye) + face_y * np.kron(np.eye(n_depth), cycle)
    return np.linalg.inv(base)


def vmem(count):
    return [pl.BlockSpec(memory_space=pltpu.VMEM)] * count


def shards(external_load, modulus, active):
    nx, ny, nz = modulus.shape
    depth_index = lax.axis_index("body")
    across_index = lax.axis_index("surf")
    n_depth = lax.axis_size("body")
    n_across = lax.axis_size("surf")
    total = n_depth * n_across
    own_index = depth_index * n_across + across_index
    inner = (depth_index > 0).astype(jnp.float32)
    mask = active.astype(jnp.float32) * (1.0 - inner)
    f32 = jnp.float32
    hi = lax.Precision.HIGHEST
    inverse = coarse_constants(n_depth, n_across, float(ny * nz), float(nx * nz))
    inv = jnp.asarray(inverse, f32)
    load = external_load.reshape(3, nx, ny, SUB, LANE)
    mod = modulus.reshape(nx, ny, SUB, LANE)
    mask = mask.reshape(ny, SUB, LANE)

    sums = jnp.concatenate([jnp.sum(load, axis=(1, 2, 3, 4)), jnp.sum(mask)[None]])
    gathered = lax.all_gather(sums[None], ("body", "surf"), axis=0, tiled=True)
    counts = gathered[:, 3]
    root = jnp.sqrt(counts[:n_across])
    small = jnp.eye(n_across, dtype=f32) + root[:, None] * inv[:n_across, :n_across] * root[None, :]
    work = jnp.concatenate([small, jnp.eye(n_across, dtype=f32)], 1)
    for k in range(n_across):
        pivot = work[k] / work[k, k]
        work = (work - work[:, k : k + 1] * pivot[None]).at[k].set(pivot)
    left = inv[:, :n_across] * root[None, :]
    normal = inv - jnp.dot(left, jnp.dot(work[:, n_across:], left.T, precision=hi), precision=hi)

    def coarse_solve(rhs):
        a = jnp.dot(normal, rhs[:, 0:1], precision=hi)
        b = jnp.dot(inv, rhs[:, 1:3], precision=hi)
        return jnp.concatenate([a, b], 1)

    def constants(alpha):
        grid = alpha.reshape(n_depth, n_across, 3)
        below = jnp.concatenate([grid[1:], jnp.zeros((1, n_across, 3), f32)], 0)
        along_x = grid - below
        along_y = grid - jnp.roll(grid, -1, axis=1)
        return along_x, along_y

    def lift(alpha):
        along_x, along_y = constants(alpha)
        zero_row = jnp.zeros((1, n_across, 3), f32)
        above = jnp.concatenate([zero_row, along_x[:-1]], 0)
        lefts = jnp.roll(along_y, 1, axis=1)
        table = jnp.concatenate([along_x, above, along_y, lefts, alpha.reshape(n_depth, n_across, 3)], 2)
        mine = lax.dynamic_slice_in_dim(table.reshape(total, 15), own_index, 1, 0)[0]

        def wide(c, n):
            return jnp.broadcast_to(c[:, None, None, None], (3, n, SUB, LANE))

        return (wide(mine[0:3], ny), wide(mine[3:6], ny), wide(mine[6:9], nx),
                wide(mine[9:12], nx), -mine[12] * mask)

    own_count = jnp.sum(mask)

    def statistics(v):
        sx = jnp.sum(v[0], axis=(1, 2, 3))
        sy = jnp.sum(v[2], axis=(1, 2, 3))
        sc = jnp.sum(v[4])
        cx = v[0] - (sx / (ny * nz))[:, None, None, None]
        cy = v[2] - (sy / (nx * nz))[:, None, None, None]
        cc = v[4] - sc / jnp.maximum(own_count, 1.0) * mask
        ss = jnp.sum(cx * cx) + jnp.sum(cy * cy) + jnp.sum(cc * cc)
        return jnp.concatenate([sx, sy, sc[None], ss[None]])

    def own_dot(a, b):
        return jnp.sum(a[0] * b[0]) + jnp.sum(a[2] * b[2]) + jnp.sum(a[4] * b[4])

    def projection(table):
        sx = table[:, 0:3].reshape(n_depth, n_across, 3)
        sy = table[:, 3:6].reshape(n_depth, n_across, 3)
        sc = table[:, 6]
        above = jnp.concatenate([jnp.zeros((1, n_across, 3), f32), sx[:-1]], 0)
        rhs = (sx - above + sy - jnp.roll(sy, 1, axis=1)).reshape(total, 3)
        rhs = rhs.at[:, 0].add(-sc)
        alpha = coarse_solve(rhs)
        along_x, along_y = constants(alpha)
        ex = sx / (ny * nz) - along_x
        ey = sy / (nx * nz) - along_y
        ec = sc / jnp.maximum(counts, 1.0) + alpha[:, 0]
        norm = (jnp.sum(table[:, 7]) + (ny * nz) * jnp.sum(ex * ex)
                + (nx * nz) * jnp.sum(ey * ey) + jnp.sum(counts * ec * ec))
        return alpha, norm

    def axpy(a, b, s):
        return tuple(x + s * y for x, y in zip(a, b))

    def gather(values):
        return lax.all_gather(values[None], ("body", "surf"), axis=0, tiled=True)

    x_shape = jax.ShapeDtypeStruct((3, ny, SUB, LANE), f32)
    y_shape = jax.ShapeDtypeStruct((3, nx, SUB, LANE), f32)
    faces = (x_shape, x_shape, y_shape, y_shape)
    iterate = pltpu.VMEM((3, nx + 2, ny + 2, SUB, LANE), f32)
    source = pltpu.VMEM((3, nx, ny, SUB, LANE), f32)
    params = pltpu.CompilerParams(vmem_limit_bytes=56 * 1024 * 1024)
    first_call = pl.pallas_call(
        functools.partial(load_kernel, nx, ny),
        out_shape=(jax.ShapeDtypeStruct((26, nx, ny, SUB, LANE), f32),
                   jax.ShapeDtypeStruct((nx, ny, SUB, LANE), f32)) + faces,
        in_specs=vmem(8), out_specs=tuple(vmem(6)),
        scratch_shapes=[pltpu.VMEM((nx + 2, ny + 2, SUB, LANE), f32), iterate, iterate, source],
        compiler_params=params,
    )
    later_call = pl.pallas_call(
        functools.partial(direction_kernel, nx, ny),
        out_shape=faces, in_specs=vmem(8), out_specs=tuple(vmem(4)),
        scratch_shapes=[iterate, iterate, source],
        compiler_params=params,
    )

    def jumps(first_x, last_x, first_y, last_y):
        pairs = [(b, b + 1) for b in range(n_depth - 1)]
        ring = [(b, (b + 1) % n_across) for b in range(n_across)]
        back = lambda p: [(t, s) for s, t in p]
        from_above = lax.ppermute(last_x, "body", pairs)
        from_below = lax.ppermute(first_x, "body", back(pairs))
        from_left = lax.ppermute(last_y, "surf", ring)
        from_right = lax.ppermute(first_y, "surf", back(ring))
        return (last_x - from_below, inner * (from_above - first_x), last_y - from_right,
                from_left - first_y, -first_x[0] * mask)

    multipliers = lift(coarse_solve(gathered[:, 0:3]))
    outs = first_call(load, mod, *multipliers, mask)
    weights, q = outs[0], outs[1]
    gradient = tuple(-piece for piece in jumps(*outs[2:]))
    alpha, rr = projection(gather(statistics(gradient)))
    residual = axpy(gradient, lift(alpha), -1.0)
    direction = residual
    for step_index in range(ITERS):
        f = later_call(weights, q, *direction, mask)
        local = (jnp.sum(direction[0] * f[1]) - jnp.sum(direction[1] * f[0])
                 + jnp.sum(direction[2] * f[3]) - jnp.sum(direction[3] * f[2])
                 - jnp.sum(direction[4] * f[0][0] * mask))
        if step_index + 1 == ITERS:
            bottom = jnp.sum(gather(local[None]))
            multipliers = axpy(multipliers, direction, rr / bottom)
            break
        image = jumps(*f)
        table = gather(jnp.concatenate(
            [statistics(image), local[None], own_dot(residual, image)[None]]))
        step = rr / jnp.sum(table[:, 8])
        alpha, ii = projection(table)
        new = rr + 2.0 * step * jnp.sum(table[:, 9]) + step * step * ii
        multipliers = axpy(multipliers, direction, step)
        residual = axpy(residual, axpy(image, lift(alpha), -1.0), step)
        direction = axpy(residual, direction, new / rr)
        rr = new
    return (multipliers[0].reshape(3, 1, ny, nz), multipliers[2].reshape(3, nx, 1, nz),
            multipliers[4].reshape(1, ny, nz))


def solution(mesh):
    placed = (P(None, "body", "surf", None), P("body", "surf", None), P("surf", None))
    return jax.shard_map(
        shards,
        mesh=mesh,
        in_specs=placed,
        out_specs=(
            P(None, "body", "surf", None),
            P(None, "body", "surf", None),
            P("body", "surf", None),
        ),
        check_vma=False,
    )
```

```python
import functools

import jax
import jax.numpy as jnp
import numpy as np
from jax import lax
from jax.experimental import pallas as pl
from jax.experimental.pallas import tpu as pltpu
from jax.sharding import PartitionSpec as P

ITERS = 3
SWEEPS = 6
COUPLING_SCALE = (0.0, 1.0, 0.5, 0.25)
RELAXATION = 0.6
PLANE = [(dx, dy) for dx in (-1, 0, 1) for dy in (-1, 0, 1)]
SAME = [o for o in PLANE if o != (0, 0)]
SUB, LANE = 8, 128


def shift_up(t):
    lane = lax.broadcasted_iota(jnp.int32, t.shape, 1)
    r = pltpu.roll(t, 1, 1)
    return jnp.where(lane == 0, pltpu.roll(r, 1, 0), r)


def shift_down(t):
    lane = lax.broadcasted_iota(jnp.int32, t.shape, 1)
    r = pltpu.roll(t, LANE - 1, 1)
    return jnp.where(lane == LANE - 1, pltpu.roll(r, SUB - 1, 0), r)


def setup_weights(nx, ny, mod_ref, mp, w_ref, q_ref):
    zero = jnp.zeros((SUB, LANE), jnp.float32)

    def clear(y, c):
        mp[0, y] = zero
        mp[nx + 1, y] = zero
        return c

    lax.fori_loop(0, ny + 2, clear, 0)

    def fill(x, c):
        mp[x + 1, 0] = zero
        mp[x + 1, ny + 1] = zero
        mp[x + 1, pl.ds(1, ny)] = mod_ref[x]
        return c

    lax.fori_loop(0, nx, fill, 0)
    sub = lax.broadcasted_iota(jnp.int32, (SUB, LANE), 0)
    lane = lax.broadcasted_iota(jnp.int32, (SUB, LANE), 1)
    first = (sub == 0) & (lane == 0)
    last = (sub == SUB - 1) & (lane == LANE - 1)

    def column(i, c):
        x = i // ny
        y = i % ny
        a = mp[x + 1, y + 1]
        up = jnp.where(first, 0.0, shift_up(a))
        down = jnp.where(last, 0.0, shift_down(a))
        total0 = zero
        total_p = zero
        total_m = zero
        for dx, dy in PLANE:
            b = mp[x + 1 + dx, y + 1 + dy]
            k = abs(dx) + abs(dy)
            if k:
                w = (2.0 * COUPLING_SCALE[k]) * a * b / (a + b)
                w_ref[SAME.index((dx, dy)), x, y] = w
                total0 = total0 + w
            scale = 2.0 * COUPLING_SCALE[k + 1]
            j = PLANE.index((dx, dy))
            w = scale * up * b / jnp.maximum(up + b, 1e-30)
            w_ref[8 + j, x, y] = w
            total_p = total_p + w
            w = scale * down * b / jnp.maximum(down + b, 1e-30)
            w_ref[17 + j, x, y] = w
            total_m = total_m + w
        diag = total0 + shift_down(total_p) + shift_up(total_m)
        q_ref[x, y] = RELAXATION / diag
        return c

    lax.fori_loop(0, nx * ny, column, 0)


def column_update(x, y, src, dst, s_ref, w_ref, q_ref):
    center, plus, minus, mid = [], [], [], []
    for comp in range(3):
        mid.append(s_ref[comp, x, y])
    for n, (dx, dy) in enumerate(PLANE):
        wp = w_ref[8 + n, x, y]
        wm = w_ref[17 + n, x, y]
        w0 = w_ref[SAME.index((dx, dy)), x, y] if (dx, dy) != (0, 0) else None
        for comp in range(3):
            v = src[comp, x + 1 + dx, y + 1 + dy]
            if n == 0:
                plus.append(wp * v)
                minus.append(wm * v)
            else:
                plus[comp] = plus[comp] + wp * v
                minus[comp] = minus[comp] + wm * v
            if w0 is None:
                center.append(v)
            else:
                mid[comp] = mid[comp] + w0 * v
    q = q_ref[x, y]
    for comp in range(3):
        total = mid[comp] + shift_down(plus[comp]) + shift_up(minus[comp])
        dst[comp, x + 1, y + 1] = (1.0 - RELAXATION) * center[comp] + q * total


def sweep(nx, ny, depth, src, dst, s_ref, w_ref, q_ref):
    full = min(nx, 2 * (depth + 1))
    step = 4

    def rows(i, c):
        r = i // (ny // step)
        y0 = (i % (ny // step)) * step
        x = r if full == nx else jnp.where(r <= depth, r, r + (nx - full))
        for j in range(step):
            column_update(x, y0 + j, src, dst, s_ref, w_ref, q_ref)
        return c

    lax.fori_loop(0, full * (ny // step), rows, 0)
    if full < nx:
        def sides(i, c):
            x = depth + 1 + i
            for j in range(depth + 1):
                column_update(x, j, src, dst, s_ref, w_ref, q_ref)
                column_update(x, ny - 1 - j, src, dst, s_ref, w_ref, q_ref)
            return c

        lax.fori_loop(0, nx - full, sides, 0)


def relax(nx, ny, local, va, vb, s_ref, w_ref, q_ref):
    deepest = (min(nx, ny) - 1) // 2

    def start(x, c):
        for comp in range(3):
            va[comp, x + 1, pl.ds(1, ny)] = q_ref[x] * s_ref[comp, x]
            if local:
                vb[comp, x + 1, pl.ds(1, ny)] = jnp.zeros((ny, SUB, LANE), jnp.float32)
        return c

    lax.fori_loop(0, nx, start, 0)
    bufs = (va, vb)
    for k in range(1, SWEEPS):
        depth = min(deepest, SWEEPS - 1 - k)
        if local:
            depth = min(depth, k)
        sweep(nx, ny, depth, bufs[(k - 1) % 2], bufs[k % 2], s_ref, w_ref, q_ref)
    return bufs[(SWEEPS - 1) % 2]


def clear_halo(nx, ny, va, vb):
    zero = jnp.zeros((SUB, LANE), jnp.float32)
    for v in (va, vb):
        for comp in range(3):
            v[comp, 0] = jnp.zeros((ny + 2, SUB, LANE), jnp.float32)
            v[comp, nx + 1] = jnp.zeros((ny + 2, SUB, LANE), jnp.float32)

            def side(x, c):
                v[comp, x + 1, 0] = zero
                v[comp, x + 1, ny + 1] = zero
                return c

            lax.fori_loop(0, nx, side, 0)


def add_faces(nx, ny, s_ref, own_x, up_x, own_y, left_y, contact, mask, sign):
    for comp in range(3):
        s_ref[comp, nx - 1] = s_ref[comp, nx - 1] + sign * own_x[comp]
        s_ref[comp, 0] = s_ref[comp, 0] - sign * up_x[comp]

        def side(x, c):
            s_ref[comp, x, ny - 1] = s_ref[comp, x, ny - 1] + sign * own_y[comp, x]
            s_ref[comp, x, 0] = s_ref[comp, x, 0] - sign * left_y[comp, x]
            return c

        lax.fori_loop(0, nx, side, 0)
    s_ref[0, 0] = s_ref[0, 0] - sign * contact[...] * mask[...]


def coarse_constants(n_depth, n_across, face_x, face_y):
    path = 2.0 * np.eye(n_depth) - np.eye(n_depth, k=1) - np.eye(n_depth, k=-1)
    path[0, 0] = 1.0
    eye = np.eye(n_across)
    cycle = 2.0 * eye - np.roll(eye, 1, axis=1) - np.roll(eye, -1, axis=1)
    base = face_x * np.kron(path, eye) + face_y * np.kron(np.eye(n_depth), cycle)
    part_x = np.kron(np.eye(n_depth) - np.eye(n_depth, k=-1), eye)
    part_y = np.kron(np.eye(n_depth), eye - np.roll(eye, 1, axis=0))
    return np.stack([part_x, part_y, part_x.T, part_y.T, np.linalg.inv(base)])


def dot(a, b):
    return jnp.dot(a, b, precision=lax.Precision.HIGHEST, preferred_element_type=jnp.float32)


def one(value):
    return jnp.sum(jnp.sum(value, axis=0, keepdims=True), axis=1, keepdims=True)


def whole(value):
    return one(jnp.sum(value.reshape((-1, SUB, LANE)), axis=0))


def feti_kernel(nx, ny, nz, n_depth, n_across, load, mod, mask, maps,
                mult_x, mult_y, mult_c, mp, va, vb, s_ref, w_ref, q_ref,
                res_x, res_y, res_c, dir_x, dir_y, dir_c, im_x, im_y, im_c, up_x, up_y,
                below_in, above_in, right_in, left_in, sent, table,
                face_send, face_recv, row_send, row_recv):
    f32 = jnp.float32
    total = n_depth * n_across
    body = lax.axis_index("body")
    surf = lax.axis_index("surf")
    me = body * n_across + surf
    below = lax.rem(body + 1, n_depth)
    above = lax.rem(body + n_depth - 1, n_depth)
    right = lax.rem(surf + 1, n_across)
    left = lax.rem(surf + n_across - 1, n_across)
    mesh_id = pl.DeviceIdType.MESH
    inner = jnp.where(body > 0, 1.0, 0.0).astype(f32)
    outer = jnp.where(body < n_depth - 1, 1.0, 0.0).astype(f32)
    area_x, area_y = float(ny * nz), float(nx * nz)
    lane = lax.broadcasted_iota(jnp.int32, (SUB, LANE), 1)
    rows = lax.broadcasted_iota(jnp.int32, (total, LANE), 0)
    lanes = lax.broadcasted_iota(jnp.int32, (total, LANE), 1)

    barrier = pltpu.get_barrier_semaphore()

    def greet(k, c):
        peer = lax.rem(me + k, total)
        pl.semaphore_signal(barrier, inc=1, device_id=(peer // n_across, lax.rem(peer, n_across)),
                            device_id_type=mesh_id)
        return c

    lax.fori_loop(1, total, greet, 0)

    def row_copy(slot, k, peer, owner):
        return pltpu.make_async_remote_copy(
            src_ref=sent.at[slot], dst_ref=table.at[slot, owner],
            send_sem=row_send.at[slot, k], recv_sem=row_recv.at[slot, owner],
            device_id=(peer // n_across, lax.rem(peer, n_across)), device_id_type=mesh_id)

    def post(slot, values):
        row = jnp.zeros((SUB, LANE), f32)
        for k, value in enumerate(values):
            row = jnp.where(lane == k, value, row)
        sent[slot] = row
        table[slot, me] = row

        def send(k, c):
            row_copy(slot, k, lax.rem(me + k, total), me).start()
            return c

        lax.fori_loop(1, total, send, 0)

    def collect(slot):
        def wait(k, c):
            peer = lax.rem(me + k, total)
            row_copy(slot, k, peer, peer).wait()
            return c

        lax.fori_loop(1, total, wait, 0)
        return table[slot, :, 0, :]

    def face_copies():
        pairs = (
            (vb.at[:, 1, pl.ds(1, ny)], below_in, (above, surf)),
            (vb.at[:, nx, pl.ds(1, ny)], above_in, (below, surf)),
            (vb.at[:, pl.ds(1, nx), 1], right_in, (body, left)),
            (vb.at[:, pl.ds(1, nx), ny], left_in, (body, right)),
        )
        return [pltpu.make_async_remote_copy(
            src_ref=a, dst_ref=b, send_sem=face_send.at[i], recv_sem=face_recv.at[i],
            device_id=peer, device_id_type=mesh_id) for i, (a, b, peer) in enumerate(pairs)]

    def at(value, row, column):
        return one(jnp.where((rows == row) & (lanes == column), value, 0.0))

    def jumps(sign):
        copies = face_copies()
        for copy in copies:
            copy.start()
        for copy in copies:
            copy.wait()
        for comp in range(3):
            first = vb[comp, 1, pl.ds(1, ny)]
            im_x[comp] = sign * (vb[comp, nx, pl.ds(1, ny)] - outer * below_in[comp])
            up_x[comp] = sign * (inner * (above_in[comp] - first))
            im_y[comp] = sign * (vb[comp, pl.ds(1, nx), ny] - right_in[comp])
            up_y[comp] = sign * (left_in[comp] - vb[comp, pl.ds(1, nx), 1])
        im_c[...] = (-sign) * vb[0, 1, pl.ds(1, ny)] * mask[...]

    own_count = whole(mask[...])

    def statistics():
        sums = [whole(im_x[comp]) for comp in range(3)] + [whole(im_y[comp]) for comp in range(3)]
        sums.append(whole(im_c[...]))
        square = jnp.zeros((SUB, LANE), f32)
        for comp in range(3):
            cx = im_x[comp] - sums[comp] / area_x
            cy = im_y[comp] - sums[3 + comp] / area_y
            square = square + jnp.sum(cx * cx, axis=0) + jnp.sum(cy * cy, axis=0)
        cc = im_c[...] - (sums[6] / jnp.maximum(own_count, 1.0)) * mask[...]
        square = square + jnp.sum(cc * cc, axis=0)
        return sums + [one(square)]

    def own_dot(a_x, a_y, a_c):
        acc = jnp.sum(a_c[...] * im_c[...], axis=0)
        for comp in range(3):
            acc = acc + jnp.sum(a_x[comp, 0] * im_x[comp], axis=0)
            acc = acc + jnp.sum(a_y[comp, 0] * im_y[comp], axis=0)
        return one(acc)

    load_sums = [whole(jnp.sum(load[comp], axis=0)) for comp in range(3)]
    pl.semaphore_wait(barrier, total - 1)
    post(0, load_sums + [own_count])
    setup_weights(nx, ny, mod, mp, w_ref, q_ref)
    clear_halo(nx, ny, va, vb)
    s_ref[...] = load[...]
    begin = collect(0)
    counts = begin[:, 3:4]

    corner = maps[4, 0:n_across, 0:n_across]
    count_face = counts[0:n_across]
    sq_row = lax.broadcasted_iota(jnp.int32, (n_across, n_across), 0)
    sq_col = lax.broadcasted_iota(jnp.int32, (n_across, n_across), 1)
    work = jnp.where(sq_row == sq_col, 1.0, 0.0) + count_face * corner
    other = jnp.where(sq_row == sq_col, count_face, 0.0)
    row_id = lax.broadcasted_iota(jnp.int32, (n_across, 1), 0)
    for k in range(n_across):
        scale = 1.0 / work[k : k + 1, k : k + 1]
        pivot, tail = work[k : k + 1] * scale, other[k : k + 1] * scale
        factor = work[:, k : k + 1]
        work = jnp.where(row_id == k, pivot, work - factor * pivot)
        other = jnp.where(row_id == k, tail, other - factor * tail)

    def coarse_solve(rhs):
        tangent = dot(maps[4], rhs)
        small = jnp.zeros((n_across, LANE), f32)
        for k in range(n_across):
            small = small + other[:, k : k + 1] * tangent[k : k + 1]
        fix = jnp.zeros((total, LANE), f32)
        for k in range(n_across):
            fix = fix + maps[4, :, k : k + 1] * small[k : k + 1]
        return jnp.where(lanes == 0, tangent - fix, tangent)

    def lifted(alpha):
        along_x = dot(maps[2], alpha)
        along_y = dot(maps[3], alpha)
        own = [[at(along_x, me, c) for c in range(3)],
               [inner * at(along_x, above * n_across + surf, c) for c in range(3)],
               [at(along_y, me, c) for c in range(3)],
               [at(along_y, body * n_across + left, c) for c in range(3)],
               at(alpha, me, 0)]
        return along_x, along_y, own

    def project(tab):
        by_x = dot(maps[0], tab)
        by_y = dot(maps[1], tab)
        rhs = by_x + pltpu.roll(by_y, LANE - 3, 1)
        rhs = rhs - jnp.where(lanes == 0, pltpu.roll(tab, LANE - 6, 1), 0.0)
        alpha = coarse_solve(jnp.where(lanes < 3, rhs, 0.0))
        along_x, along_y, own = lifted(alpha)
        ex = jnp.where(lanes < 3, tab / area_x - along_x, 0.0)
        ey = jnp.where(lanes < 3, pltpu.roll(tab, LANE - 3, 1) / area_y - along_y, 0.0)
        ec = tab[:, 6:7] / jnp.maximum(counts, 1.0) + alpha[:, 0:1]
        norm = one(jnp.where(lanes == 7, tab, 0.0) + area_x * ex * ex + area_y * ey * ey
                   + jnp.where(lanes == 0, counts * ec * ec, 0.0))
        for comp in range(3):
            im_x[comp] = im_x[comp] - own[0][comp]
            up_x[comp] = up_x[comp] - own[1][comp]
            im_y[comp] = im_y[comp] - own[2][comp]
            up_y[comp] = up_y[comp] - own[3][comp]
        im_c[...] = im_c[...] + own[4] * mask[...]
        return norm

    own = lifted(coarse_solve(jnp.where(lanes < 3, begin, 0.0)))[2]
    for comp in range(3):
        dir_x[comp, 0] = jnp.broadcast_to(own[0][comp], (ny, SUB, LANE))
        dir_x[comp, 1] = jnp.broadcast_to(own[1][comp], (ny, SUB, LANE))
        dir_y[comp, 0] = jnp.broadcast_to(own[2][comp], (nx, SUB, LANE))
        dir_y[comp, 1] = jnp.broadcast_to(own[3][comp], (nx, SUB, LANE))
        mult_x[comp] = dir_x[comp, 0]
        mult_y[comp] = dir_y[comp, 0]
    dir_c[...] = -own[4] * mask[...]
    mult_c[...] = dir_c[...]

    def put_faces(sign):
        add_faces(nx, ny, s_ref, dir_x.at[:, 0], dir_x.at[:, 1], dir_y.at[:, 0], dir_y.at[:, 1],
                  dir_c, mask, sign)

    put_faces(-1.0)
    relax(nx, ny, False, va, vb, s_ref, w_ref, q_ref)
    jumps(-1.0)
    post(1, statistics())
    rr = project(collect(1))
    for comp in range(3):
        for k, (a, b) in enumerate(((im_x, im_y), (up_x, up_y))):
            res_x[comp, k] = a[comp]
            dir_x[comp, k] = a[comp]
            res_y[comp, k] = b[comp]
            dir_y[comp, k] = b[comp]
    res_c[...] = im_c[...]
    dir_c[...] = im_c[...]

    def climb(step):
        for comp in range(3):
            mult_x[comp] = mult_x[comp] + step * dir_x[comp, 0]
            mult_y[comp] = mult_y[comp] + step * dir_y[comp, 0]
        mult_c[...] = mult_c[...] + step * dir_c[...]

    for iteration in range(ITERS):
        slot = iteration % 2
        s_ref[...] = jnp.zeros_like(s_ref)
        put_faces(1.0)
        relax(nx, ny, True, va, vb, s_ref, w_ref, q_ref)
        if iteration + 1 == ITERS:
            acc = -jnp.sum(dir_c[...] * vb[0, 1, pl.ds(1, ny)] * mask[...], axis=0)
            for comp in range(3):
                acc = acc + jnp.sum(dir_x[comp, 0] * vb[comp, nx, pl.ds(1, ny)], axis=0)
                acc = acc - jnp.sum(dir_x[comp, 1] * vb[comp, 1, pl.ds(1, ny)], axis=0)
                acc = acc + jnp.sum(dir_y[comp, 0] * vb[comp, pl.ds(1, nx), ny], axis=0)
                acc = acc - jnp.sum(dir_y[comp, 1] * vb[comp, pl.ds(1, nx), 1], axis=0)
            post(slot, [one(acc)])
            bottom = one(jnp.where(lanes == 0, collect(slot), 0.0))
            climb(rr / bottom)
            break
        jumps(1.0)
        post(slot, statistics() + [own_dot(dir_x, dir_y, dir_c), own_dot(res_x, res_y, res_c)])
        tab = collect(slot)
        norm = project(tab)
        step = rr / one(jnp.where(lanes == 8, tab, 0.0))
        cross = one(jnp.where(lanes == 9, tab, 0.0))
        new = rr + 2.0 * step * cross + step * step * norm
        climb(step)
        beta = new / rr
        for comp in range(3):
            for k, (a, b) in enumerate(((im_x, im_y), (up_x, up_y))):
                value = res_x[comp, k] + step * a[comp]
                res_x[comp, k] = value
                dir_x[comp, k] = value + beta * dir_x[comp, k]
                value = res_y[comp, k] + step * b[comp]
                res_y[comp, k] = value
                dir_y[comp, k] = value + beta * dir_y[comp, k]
        value = res_c[...] + step * im_c[...]
        res_c[...] = value
        dir_c[...] = value + beta * dir_c[...]
        rr = new


def shards(external_load, modulus, active):
    nx, ny, nz = modulus.shape
    n_depth = lax.axis_size("body")
    n_across = lax.axis_size("surf")
    total = n_depth * n_across
    f32 = jnp.float32
    top = (lax.axis_index("body") == 0).astype(f32)
    mask = (active.astype(f32) * top).reshape(ny, SUB, LANE)
    maps = jnp.asarray(coarse_constants(n_depth, n_across, float(ny * nz), float(nx * nz)), f32)
    spec = pl.BlockSpec(memory_space=pltpu.VMEM)
    face_x, face_y, tiles = (3, ny, SUB, LANE), (3, nx, SUB, LANE), (ny, SUB, LANE)
    two_x, two_y = (3, 2, ny, SUB, LANE), (3, 2, nx, SUB, LANE)
    iterate = (3, nx + 2, ny + 2, SUB, LANE)
    shapes = [(nx + 2, ny + 2, SUB, LANE), iterate, iterate, (3, nx, ny, SUB, LANE),
              (26, nx, ny, SUB, LANE), (nx, ny, SUB, LANE),
              two_x, two_y, tiles, two_x, two_y, tiles, face_x, face_y, tiles, face_x, face_y,
              face_x, face_x, face_y, face_y, (2, SUB, LANE), (2, total, SUB, LANE)]
    out = pl.pallas_call(
        functools.partial(feti_kernel, nx, ny, nz, n_depth, n_across),
        out_shape=tuple(jax.ShapeDtypeStruct(s, f32) for s in (face_x, face_y, tiles)),
        in_specs=[spec] * 4, out_specs=(spec,) * 3,
        scratch_shapes=[pltpu.VMEM(s, f32) for s in shapes] + [
            pltpu.SemaphoreType.DMA((4,)), pltpu.SemaphoreType.DMA((4,)),
            pltpu.SemaphoreType.DMA((2, total)), pltpu.SemaphoreType.DMA((2, total))],
        compiler_params=pltpu.CompilerParams(
            vmem_limit_bytes=56 * 1024 * 1024, collective_id=0, has_side_effects=True),
    )(external_load.reshape(3, nx, ny, SUB, LANE), modulus.reshape(nx, ny, SUB, LANE), mask, maps)
    return (out[0].reshape(3, 1, ny, nz), out[1].reshape(3, nx, 1, nz), out[2].reshape(1, ny, nz))


def solution(mesh):
    placed = (P(None, "body", "surf", None), P("body", "surf", None), P("surf", None))
    return jax.shard_map(
        shards,
        mesh=mesh,
        in_specs=placed,
        out_specs=(
            P(None, "body", "surf", None),
            P(None, "body", "surf", None),
            P("body", "surf", None),
        ),
        check_vma=False,
    )
```

```python
import functools

import jax
import jax.numpy as jnp
import numpy as np
from jax import lax
from jax.experimental import pallas as pl
from jax.experimental.pallas import tpu as pltpu
from jax.sharding import PartitionSpec as P

ITERS = 3
SWEEPS = 6
COUPLING_SCALE = (0.0, 1.0, 0.5, 0.25)
RELAXATION = 0.6
PLANE = [(dx, dy) for dx in (-1, 0, 1) for dy in (-1, 0, 1)]
SAME = [o for o in PLANE if o != (0, 0)]
SUB, LANE = 8, 128


def shift_up(t):
    lane = lax.broadcasted_iota(jnp.int32, t.shape, 1)
    r = pltpu.roll(t, 1, 1)
    return jnp.where(lane == 0, pltpu.roll(r, 1, 0), r)


def shift_down(t):
    lane = lax.broadcasted_iota(jnp.int32, t.shape, 1)
    r = pltpu.roll(t, LANE - 1, 1)
    return jnp.where(lane == LANE - 1, pltpu.roll(r, SUB - 1, 0), r)


def setup_weights(nx, ny, mod_ref, mp, w_ref, q_ref):
    zero = jnp.zeros((SUB, LANE), jnp.float32)

    def clear(y, c):
        mp[0, y] = zero
        mp[nx + 1, y] = zero
        return c

    lax.fori_loop(0, ny + 2, clear, 0)

    def fill(x, c):
        mp[x + 1, 0] = zero
        mp[x + 1, ny + 1] = zero
        mp[x + 1, pl.ds(1, ny)] = mod_ref[x]
        return c

    lax.fori_loop(0, nx, fill, 0)
    sub = lax.broadcasted_iota(jnp.int32, (SUB, LANE), 0)
    lane = lax.broadcasted_iota(jnp.int32, (SUB, LANE), 1)
    first = (sub == 0) & (lane == 0)
    last = (sub == SUB - 1) & (lane == LANE - 1)

    def column(x, y):
        a = mp[x + 1, y + 1]
        up = jnp.where(first, 0.0, shift_up(a))
        down = jnp.where(last, 0.0, shift_down(a))
        total0 = zero
        total_p = zero
        total_m = zero
        for dx, dy in PLANE:
            b = mp[x + 1 + dx, y + 1 + dy]
            k = abs(dx) + abs(dy)
            if k:
                w = (2.0 * COUPLING_SCALE[k]) * a * b / (a + b)
                w_ref[SAME.index((dx, dy)), x, y] = w
                total0 = total0 + w
            scale = 2.0 * COUPLING_SCALE[k + 1]
            j = PLANE.index((dx, dy))
            w = scale * up * b / jnp.maximum(up + b, 1e-30)
            w_ref[8 + j, x, y] = w
            total_p = total_p + w
            w = scale * down * b / jnp.maximum(down + b, 1e-30)
            w_ref[17 + j, x, y] = w
            total_m = total_m + w
        diag = total0 + shift_down(total_p) + shift_up(total_m)
        q_ref[x, y] = RELAXATION / diag

    batch = 8

    def columns(i, c):
        per_row = ny // batch
        for j in range(batch):
            column(i // per_row, lax.rem(i, per_row) * batch + j)
        return c

    lax.fori_loop(0, nx * ny // batch, columns, 0)


def column_update(x, y, src, dst, s_ref, w_ref, q_ref):
    center, plus, minus, mid = [], [], [], []
    for comp in range(3):
        mid.append(s_ref[comp, x, y])
    for n, (dx, dy) in enumerate(PLANE):
        wp = w_ref[8 + n, x, y]
        wm = w_ref[17 + n, x, y]
        w0 = w_ref[SAME.index((dx, dy)), x, y] if (dx, dy) != (0, 0) else None
        for comp in range(3):
            v = src[comp, x + 1 + dx, y + 1 + dy]
            if n == 0:
                plus.append(wp * v)
                minus.append(wm * v)
            else:
                plus[comp] = plus[comp] + wp * v
                minus[comp] = minus[comp] + wm * v
            if w0 is None:
                center.append(v)
            else:
                mid[comp] = mid[comp] + w0 * v
    q = q_ref[x, y]
    for comp in range(3):
        total = mid[comp] + shift_down(plus[comp]) + shift_up(minus[comp])
        dst[comp, x + 1, y + 1] = (1.0 - RELAXATION) * center[comp] + q * total


def sweep(nx, ny, depth, src, dst, s_ref, w_ref, q_ref):
    full = min(nx, 2 * (depth + 1))
    step = 8

    def rows(i, c):
        r = i // (ny // step)
        y0 = (i % (ny // step)) * step
        x = r if full == nx else jnp.where(r <= depth, r, r + (nx - full))
        for j in range(step):
            column_update(x, y0 + j, src, dst, s_ref, w_ref, q_ref)
        return c

    lax.fori_loop(0, full * (ny // step), rows, 0)
    if full < nx:
        batch = max(b for b in (1, 2, 3) if (nx - full) % b == 0 and b * (depth + 1) <= 4 or b == 1)

        def sides(i, c):
            for k in range(batch):
                x = depth + 1 + i * batch + k
                for j in range(depth + 1):
                    column_update(x, j, src, dst, s_ref, w_ref, q_ref)
                    column_update(x, ny - 1 - j, src, dst, s_ref, w_ref, q_ref)
            return c

        lax.fori_loop(0, (nx - full) // batch, sides, 0)


def relax(nx, ny, local, va, vb, s_ref, w_ref, q_ref):
    deepest = (min(nx, ny) - 1) // 2

    def start(x, c):
        for comp in range(3):
            va[comp, x + 1, pl.ds(1, ny)] = q_ref[x] * s_ref[comp, x]
            if local:
                vb[comp, x + 1, pl.ds(1, ny)] = jnp.zeros((ny, SUB, LANE), jnp.float32)
        return c

    lax.fori_loop(0, nx, start, 0)
    bufs = (va, vb)
    for k in range(1, SWEEPS):
        depth = min(deepest, SWEEPS - 1 - k)
        if local:
            depth = min(depth, k)
        sweep(nx, ny, depth, bufs[(k - 1) % 2], bufs[k % 2], s_ref, w_ref, q_ref)
    return bufs[(SWEEPS - 1) % 2]


def clear_halo(nx, ny, va, vb):
    zero = jnp.zeros((SUB, LANE), jnp.float32)
    for v in (va, vb):
        for comp in range(3):
            v[comp, 0] = jnp.zeros((ny + 2, SUB, LANE), jnp.float32)
            v[comp, nx + 1] = jnp.zeros((ny + 2, SUB, LANE), jnp.float32)

            def side(x, c):
                v[comp, x + 1, 0] = zero
                v[comp, x + 1, ny + 1] = zero
                return c

            lax.fori_loop(0, nx, side, 0)


def add_faces(nx, ny, s_ref, own_x, up_x, own_y, left_y, contact, mask, sign):
    for comp in range(3):
        s_ref[comp, nx - 1] = s_ref[comp, nx - 1] + sign * own_x[comp]
        s_ref[comp, 0] = s_ref[comp, 0] - sign * up_x[comp]

        def side(x, c):
            s_ref[comp, x, ny - 1] = s_ref[comp, x, ny - 1] + sign * own_y[comp, x]
            s_ref[comp, x, 0] = s_ref[comp, x, 0] - sign * left_y[comp, x]
            return c

        lax.fori_loop(0, nx, side, 0)
    s_ref[0, 0] = s_ref[0, 0] - sign * contact[...] * mask[...]


def coarse_constants(n_depth, n_across, face_x, face_y):
    path = 2.0 * np.eye(n_depth) - np.eye(n_depth, k=1) - np.eye(n_depth, k=-1)
    path[0, 0] = 1.0
    eye = np.eye(n_across)
    cycle = 2.0 * eye - np.roll(eye, 1, axis=1) - np.roll(eye, -1, axis=1)
    base = face_x * np.kron(path, eye) + face_y * np.kron(np.eye(n_depth), cycle)
    part_x = np.kron(np.eye(n_depth) - np.eye(n_depth, k=-1), eye)
    part_y = np.kron(np.eye(n_depth), eye - np.roll(eye, 1, axis=0))
    return np.stack([part_x, part_y, part_x.T, part_y.T, np.linalg.inv(base)])


def dot(a, b):
    return jnp.dot(a, b, precision=lax.Precision.HIGHEST, preferred_element_type=jnp.float32)


def one(value):
    return jnp.sum(jnp.sum(value, axis=0, keepdims=True), axis=1, keepdims=True)


def whole(value):
    return one(jnp.sum(value.reshape((-1, SUB, LANE)), axis=0))


def feti_kernel(nx, ny, nz, n_depth, n_across, load, mod, mask, maps,
                mult_x, mult_y, mult_c, mp, va, vb, s_ref, w_ref, q_ref,
                res_x, res_y, res_c, dir_x, dir_y, dir_c, im_x, im_y, im_c, up_x, up_y,
                below_in, above_in, right_in, left_in, sent, table,
                face_send, face_recv, row_send, row_recv):
    f32 = jnp.float32
    total = n_depth * n_across
    body = lax.axis_index("body")
    surf = lax.axis_index("surf")
    me = body * n_across + surf
    below = lax.rem(body + 1, n_depth)
    above = lax.rem(body + n_depth - 1, n_depth)
    right = lax.rem(surf + 1, n_across)
    left = lax.rem(surf + n_across - 1, n_across)
    mesh_id = pl.DeviceIdType.MESH
    inner = jnp.where(body > 0, 1.0, 0.0).astype(f32)
    outer = jnp.where(body < n_depth - 1, 1.0, 0.0).astype(f32)
    area_x, area_y = float(ny * nz), float(nx * nz)
    lane = lax.broadcasted_iota(jnp.int32, (SUB, LANE), 1)
    rows = lax.broadcasted_iota(jnp.int32, (total, LANE), 0)
    lanes = lax.broadcasted_iota(jnp.int32, (total, LANE), 1)

    barrier = pltpu.get_barrier_semaphore()

    peer_surf = [lax.rem(surf + k, n_across) for k in range(n_across)]

    def every_peer(act):
        for k in range(1, n_across):
            act(k, body, peer_surf[k])

        def others(d, c):
            there = lax.rem(body + d, n_depth)
            for k in range(n_across):
                act(d * n_across + k, there, peer_surf[k])
            return c

        lax.fori_loop(1, n_depth, others, 0)

    every_peer(lambda k, b, s: pl.semaphore_signal(
        barrier, inc=1, device_id=(b, s), device_id_type=mesh_id))

    def row_copy(slot, k, b, s, owner):
        return pltpu.make_async_remote_copy(
            src_ref=sent.at[slot], dst_ref=table.at[slot, owner],
            send_sem=row_send.at[slot, k], recv_sem=row_recv.at[slot, owner],
            device_id=(b, s), device_id_type=mesh_id)

    def post(slot, values):
        row = jnp.zeros((SUB, LANE), f32)
        for k, value in enumerate(values):
            row = jnp.where(lane == k, value, row)
        sent[slot] = row
        table[slot, me] = row

        every_peer(lambda k, b, s: row_copy(slot, k, b, s, me).start())

    def collect(slot):
        every_peer(lambda k, b, s: row_copy(slot, k, b, s, b * n_across + s).wait())
        return table[slot, :, 0, :]

    def face_copies():
        pairs = (
            (vb.at[:, 1, pl.ds(1, ny)], below_in, (above, surf)),
            (vb.at[:, nx, pl.ds(1, ny)], above_in, (below, surf)),
            (vb.at[:, pl.ds(1, nx), 1], right_in, (body, left)),
            (vb.at[:, pl.ds(1, nx), ny], left_in, (body, right)),
        )
        return [pltpu.make_async_remote_copy(
            src_ref=a, dst_ref=b, send_sem=face_send.at[i], recv_sem=face_recv.at[i],
            device_id=peer, device_id_type=mesh_id) for i, (a, b, peer) in enumerate(pairs)]

    def at(value, row, column):
        return one(jnp.where((rows == row) & (lanes == column), value, 0.0))

    def jumps(sign):
        copies = face_copies()
        for copy in copies:
            copy.start()
        for copy in copies:
            copy.wait()
        for comp in range(3):
            first = vb[comp, 1, pl.ds(1, ny)]
            im_x[comp] = sign * (vb[comp, nx, pl.ds(1, ny)] - outer * below_in[comp])
            up_x[comp] = sign * (inner * (above_in[comp] - first))
            im_y[comp] = sign * (vb[comp, pl.ds(1, nx), ny] - right_in[comp])
            up_y[comp] = sign * (left_in[comp] - vb[comp, pl.ds(1, nx), 1])
        im_c[...] = (-sign) * vb[0, 1, pl.ds(1, ny)] * mask[...]

    own_count = whole(mask[...])

    def statistics():
        sums = [whole(im_x[comp]) for comp in range(3)] + [whole(im_y[comp]) for comp in range(3)]
        sums.append(whole(im_c[...]))
        square = jnp.zeros((SUB, LANE), f32)
        for comp in range(3):
            cx = im_x[comp] - sums[comp] / area_x
            cy = im_y[comp] - sums[3 + comp] / area_y
            square = square + jnp.sum(cx * cx, axis=0) + jnp.sum(cy * cy, axis=0)
        cc = im_c[...] - (sums[6] / jnp.maximum(own_count, 1.0)) * mask[...]
        square = square + jnp.sum(cc * cc, axis=0)
        return sums + [one(square)]

    def own_dot(a_x, a_y, a_c):
        acc = jnp.sum(a_c[...] * im_c[...], axis=0)
        for comp in range(3):
            acc = acc + jnp.sum(a_x[comp, 0] * im_x[comp], axis=0)
            acc = acc + jnp.sum(a_y[comp, 0] * im_y[comp], axis=0)
        return one(acc)

    load_sums = [whole(jnp.sum(load[comp], axis=0)) for comp in range(3)]
    pl.semaphore_wait(barrier, total - 1)
    post(0, load_sums + [own_count])
    setup_weights(nx, ny, mod, mp, w_ref, q_ref)
    clear_halo(nx, ny, va, vb)
    s_ref[...] = load[...]
    begin = collect(0)
    counts = begin[:, 3:4]

    corner = maps[4, 0:n_across, 0:n_across]
    count_face = counts[0:n_across]
    sq_row = lax.broadcasted_iota(jnp.int32, (n_across, n_across), 0)
    sq_col = lax.broadcasted_iota(jnp.int32, (n_across, n_across), 1)
    work = jnp.where(sq_row == sq_col, 1.0, 0.0) + count_face * corner
    other = jnp.where(sq_row == sq_col, count_face, 0.0)
    row_id = lax.broadcasted_iota(jnp.int32, (n_across, 1), 0)
    for k in range(n_across):
        scale = 1.0 / work[k : k + 1, k : k + 1]
        pivot, tail = work[k : k + 1] * scale, other[k : k + 1] * scale
        factor = work[:, k : k + 1]
        work = jnp.where(row_id == k, pivot, work - factor * pivot)
        other = jnp.where(row_id == k, tail, other - factor * tail)

    def coarse_solve(rhs):
        tangent = dot(maps[4], rhs)
        small = jnp.zeros((n_across, LANE), f32)
        for k in range(n_across):
            small = small + other[:, k : k + 1] * tangent[k : k + 1]
        fix = jnp.zeros((total, LANE), f32)
        for k in range(n_across):
            fix = fix + maps[4, :, k : k + 1] * small[k : k + 1]
        return jnp.where(lanes == 0, tangent - fix, tangent)

    def lifted(alpha):
        along_x = dot(maps[2], alpha)
        along_y = dot(maps[3], alpha)
        own = [[at(along_x, me, c) for c in range(3)],
               [inner * at(along_x, above * n_across + surf, c) for c in range(3)],
               [at(along_y, me, c) for c in range(3)],
               [at(along_y, body * n_across + left, c) for c in range(3)],
               at(alpha, me, 0)]
        return along_x, along_y, own

    def project(tab):
        by_x = dot(maps[0], tab)
        by_y = dot(maps[1], tab)
        rhs = by_x + pltpu.roll(by_y, LANE - 3, 1)
        rhs = rhs - jnp.where(lanes == 0, pltpu.roll(tab, LANE - 6, 1), 0.0)
        alpha = coarse_solve(jnp.where(lanes < 3, rhs, 0.0))
        along_x, along_y, own = lifted(alpha)
        ex = jnp.where(lanes < 3, tab / area_x - along_x, 0.0)
        ey = jnp.where(lanes < 3, pltpu.roll(tab, LANE - 3, 1) / area_y - along_y, 0.0)
        ec = tab[:, 6:7] / jnp.maximum(counts, 1.0) + alpha[:, 0:1]
        norm = one(jnp.where(lanes == 7, tab, 0.0) + area_x * ex * ex + area_y * ey * ey
                   + jnp.where(lanes == 0, counts * ec * ec, 0.0))
        for comp in range(3):
            im_x[comp] = im_x[comp] - own[0][comp]
            up_x[comp] = up_x[comp] - own[1][comp]
            im_y[comp] = im_y[comp] - own[2][comp]
            up_y[comp] = up_y[comp] - own[3][comp]
        im_c[...] = im_c[...] + own[4] * mask[...]
        return norm

    own = lifted(coarse_solve(jnp.where(lanes < 3, begin, 0.0)))[2]
    for comp in range(3):
        dir_x[comp, 0] = jnp.broadcast_to(own[0][comp], (ny, SUB, LANE))
        dir_x[comp, 1] = jnp.broadcast_to(own[1][comp], (ny, SUB, LANE))
        dir_y[comp, 0] = jnp.broadcast_to(own[2][comp], (nx, SUB, LANE))
        dir_y[comp, 1] = jnp.broadcast_to(own[3][comp], (nx, SUB, LANE))
        mult_x[comp] = dir_x[comp, 0]
        mult_y[comp] = dir_y[comp, 0]
    dir_c[...] = -own[4] * mask[...]
    mult_c[...] = dir_c[...]

    def put_faces(sign):
        add_faces(nx, ny, s_ref, dir_x.at[:, 0], dir_x.at[:, 1], dir_y.at[:, 0], dir_y.at[:, 1],
                  dir_c, mask, sign)

    put_faces(-1.0)
    relax(nx, ny, False, va, vb, s_ref, w_ref, q_ref)
    jumps(-1.0)
    post(1, statistics())
    rr = project(collect(1))
    for comp in range(3):
        for k, (a, b) in enumerate(((im_x, im_y), (up_x, up_y))):
            res_x[comp, k] = a[comp]
            dir_x[comp, k] = a[comp]
            res_y[comp, k] = b[comp]
            dir_y[comp, k] = b[comp]
    res_c[...] = im_c[...]
    dir_c[...] = im_c[...]

    def climb(step):
        for comp in range(3):
            mult_x[comp] = mult_x[comp] + step * dir_x[comp, 0]
            mult_y[comp] = mult_y[comp] + step * dir_y[comp, 0]
        mult_c[...] = mult_c[...] + step * dir_c[...]

    for iteration in range(ITERS):
        slot = iteration % 2
        s_ref[...] = jnp.zeros_like(s_ref)
        put_faces(1.0)
        relax(nx, ny, True, va, vb, s_ref, w_ref, q_ref)
        if iteration + 1 == ITERS:
            acc = -jnp.sum(dir_c[...] * vb[0, 1, pl.ds(1, ny)] * mask[...], axis=0)
            for comp in range(3):
                acc = acc + jnp.sum(dir_x[comp, 0] * vb[comp, nx, pl.ds(1, ny)], axis=0)
                acc = acc - jnp.sum(dir_x[comp, 1] * vb[comp, 1, pl.ds(1, ny)], axis=0)
                acc = acc + jnp.sum(dir_y[comp, 0] * vb[comp, pl.ds(1, nx), ny], axis=0)
                acc = acc - jnp.sum(dir_y[comp, 1] * vb[comp, pl.ds(1, nx), 1], axis=0)
            post(slot, [one(acc)])
            bottom = one(jnp.where(lanes == 0, collect(slot), 0.0))
            climb(rr / bottom)
            break
        jumps(1.0)
        post(slot, statistics() + [own_dot(dir_x, dir_y, dir_c), own_dot(res_x, res_y, res_c)])
        tab = collect(slot)
        norm = project(tab)
        step = rr / one(jnp.where(lanes == 8, tab, 0.0))
        cross = one(jnp.where(lanes == 9, tab, 0.0))
        new = rr + 2.0 * step * cross + step * step * norm
        climb(step)
        beta = new / rr
        for comp in range(3):
            for k, (a, b) in enumerate(((im_x, im_y), (up_x, up_y))):
                value = res_x[comp, k] + step * a[comp]
                res_x[comp, k] = value
                dir_x[comp, k] = value + beta * dir_x[comp, k]
                value = res_y[comp, k] + step * b[comp]
                res_y[comp, k] = value
                dir_y[comp, k] = value + beta * dir_y[comp, k]
        value = res_c[...] + step * im_c[...]
        res_c[...] = value
        dir_c[...] = value + beta * dir_c[...]
        rr = new


def shards(external_load, modulus, active):
    nx, ny, nz = modulus.shape
    n_depth = lax.axis_size("body")
    n_across = lax.axis_size("surf")
    total = n_depth * n_across
    f32 = jnp.float32
    top = (lax.axis_index("body") == 0).astype(f32)
    mask = (active.astype(f32) * top).reshape(ny, SUB, LANE)
    maps = jnp.asarray(coarse_constants(n_depth, n_across, float(ny * nz), float(nx * nz)), f32)
    spec = pl.BlockSpec(memory_space=pltpu.VMEM)
    face_x, face_y, tiles = (3, ny, SUB, LANE), (3, nx, SUB, LANE), (ny, SUB, LANE)
    two_x, two_y = (3, 2, ny, SUB, LANE), (3, 2, nx, SUB, LANE)
    iterate = (3, nx + 2, ny + 2, SUB, LANE)
    shapes = [(nx + 2, ny + 2, SUB, LANE), iterate, iterate, (3, nx, ny, SUB, LANE),
              (26, nx, ny, SUB, LANE), (nx, ny, SUB, LANE),
              two_x, two_y, tiles, two_x, two_y, tiles, face_x, face_y, tiles, face_x, face_y,
              face_x, face_x, face_y, face_y, (2, SUB, LANE), (2, total, SUB, LANE)]
    out = pl.pallas_call(
        functools.partial(feti_kernel, nx, ny, nz, n_depth, n_across),
        out_shape=tuple(jax.ShapeDtypeStruct(s, f32) for s in (face_x, face_y, tiles)),
        in_specs=[spec] * 4, out_specs=(spec,) * 3,
        scratch_shapes=[pltpu.VMEM(s, f32) for s in shapes] + [
            pltpu.SemaphoreType.DMA((4,)), pltpu.SemaphoreType.DMA((4,)),
            pltpu.SemaphoreType.DMA((2, total)), pltpu.SemaphoreType.DMA((2, total))],
        compiler_params=pltpu.CompilerParams(
            vmem_limit_bytes=56 * 1024 * 1024, collective_id=0, has_side_effects=True),
    )(external_load.reshape(3, nx, ny, SUB, LANE), modulus.reshape(nx, ny, SUB, LANE), mask, maps)
    return (out[0].reshape(3, 1, ny, nz), out[1].reshape(3, nx, 1, nz), out[2].reshape(1, ny, nz))


def solution(mesh):
    placed = (P(None, "body", "surf", None), P("body", "surf", None), P("surf", None))
    return jax.shard_map(
        shards,
        mesh=mesh,
        in_specs=placed,
        out_specs=(
            P(None, "body", "surf", None),
            P(None, "body", "surf", None),
            P("body", "surf", None),
        ),
        check_vma=False,
    )
```
